32 devices in a mesh: dp: 8 (over z, x), segment: 2 (over y), mp: 2 (over core).
Axes of the slice: x: 2, y: 2, z: 4, core: 2. Of those that a mesh axis runs over, the one named last changes fastest.
Arguments:
- prefix_hidden: bfloat16 [16, 512, 8192], P(('dp', 'segment'), 'mp'), may hold values from -6 to 6
- norm_gain: float32 [8192], replicated, may hold values from 0.5 to 1.5
- kv_weight: bfloat16 [8192, 2, 1024], P('dp', None, 'mp'), may hold values from -0.0625 to 0.0625
- action_query: bfloat16 [16, 128, 2048], P(('dp', 'segment'), None, 'mp'), may hold values from -104 to 104
- action_kv: bfloat16 [16, 128, 2, 1024], P(('dp', 'segment'), None, None, 'mp'), may hold values from -4.25 to 4.25
- out_cotangent: bfloat16 [16, 128, 2048], P(('dp', 'segment'), None, 'mp'), may hold values from -18 to 18
- prefix_blocks: int32 [16, 512], P(('dp', 'segment')), may hold values from 0 to 7, as said below
- action_blocks: int32 [16, 128], P(('dp', 'segment')), may hold values from 0 to 8, as said below
- prefix_lengths: int32 [16], P(('dp', 'segment')), may hold values from 128 to 512, as said below
- timesteps: int32 [16], P(('dp', 'segment')), may hold values from 0 to 999
Outputs:
- attn_out: bfloat16 [16, 128, 2048], P(('dp', 'segment'), None, 'mp')
- query_grad: float32 [16, 128, 2048], P(('dp', 'segment'), None, 'mp')
- action_kv_grad: float32 [16, 128, 2, 1024], P(('dp', 'segment'), None, None, 'mp')
- weight_grad: float32 [8192, 2, 1024], P('dp', None, 'mp')
The draws below stay inside these ranges and needn't reach their ends.
Inputs may be any that keep to these rules, and one draw needn't show every extreme that they name: `prefix_blocks`: constant over each run of 64 positions, 0 on the first run, rising by 0 or 1 from one run to the next; in every draw some sample rises at every run. `action_blocks`: constant over each run of 64 positions; the last run of every sample holds 8; in every draw some sample's first run holds 0. `prefix_lengths`: in every draw some sample's prefix is whole and some sample's is 128.
All inputs are finite; a program needn't handle non-finite values.
Results may differ from the reference program's by a relative error of at most 0.017.
Values may be sent and summed in bfloat16 or wider, within the bound.
A program may use at most 128 MiB of HBM per device.

```python
import jax
import jax.numpy as jnp
from jax import lax

D = 8192
KVH = 8
HD = 128
QH = 16
PREFIX = 512
ACT = 128
TILE = 64
STEPS = 1000
SAMPLES = 16


def paired_actions(key):
    base = jax.random.fold_in(key, 31)
    pairs = jnp.clip(jax.random.normal(jax.random.fold_in(base, 1), (SAMPLES, ACT, 2, KVH * HD), jnp.float32), -4.0, 4.0)
    queries = jnp.clip(jax.random.normal(jax.random.fold_in(base, 2), (SAMPLES, ACT, QH * HD), jnp.float32), -4.0, 4.0)
    return (pairs, queries)


def draw_action_kv(key, part):
    return paired_actions(key)[0].astype(jnp.bfloat16)


def draw_action_query(key, part):
    return paired_actions(key)[1].astype(jnp.bfloat16)


def draw_prefix_blocks(key, part):
    tiles = PREFIX // TILE
    rises = jax.random.randint(jax.random.fold_in(key, 21), (SAMPLES, tiles), 0, 2)
    chosen = jax.random.randint(jax.random.fold_in(key, 25), (), 0, SAMPLES)
    rises = jnp.where((jnp.arange(SAMPLES) == chosen)[:, None], 1, rises)
    rises = rises.at[:, 0].set(0)
    levels = jnp.cumsum(rises, axis=1).astype(jnp.int32)
    return jnp.repeat(levels, TILE, axis=1).astype(jnp.int32)


def draw_action_blocks(key, part):
    tiles = ACT // TILE
    highest = PREFIX // TILE
    levels = jax.random.randint(jax.random.fold_in(key, 22), (SAMPLES, tiles), 0, highest + 1)
    chosen = jax.random.randint(jax.random.fold_in(key, 26), (), 0, SAMPLES)
    levels = levels.at[chosen, 0].set(0)
    levels = levels.at[:, tiles - 1].set(highest)
    return jnp.repeat(levels, TILE, axis=1).astype(jnp.int32)


def draw_prefix_lengths(key, part):
    lengths = jax.random.randint(jax.random.fold_in(key, 23), (SAMPLES,), PREFIX // 4, PREFIX + 1)
    chosen = jax.random.randint(jax.random.fold_in(key, 24), (), 0, SAMPLES)
    index = jnp.arange(SAMPLES)
    lengths = jnp.where(index == (chosen + 1) % SAMPLES, PREFIX // 4, lengths)
    return jnp.where(index == chosen, PREFIX, lengths).astype(jnp.int32)


def place_ends(entries, rng, smallest, largest):
    longest = entries.shape.index(max(entries.shape))
    spots = []
    for shift in (0, 1):
        where = [jax.random.randint(jax.random.fold_in(rng, axis), (), 0, length) for axis, length in enumerate(entries.shape)]
        where[longest] = (where[longest] + shift) % entries.shape[longest]
        spots.append(tuple(where))
    return entries.at[spots[0]].set(smallest).at[spots[1]].set(largest)


def spiked(result, stream_key, source, target, parts, factor):
    def block_of(axis_at):
        return (jnp.arange(result.shape[axis_at]) // (result.shape[axis_at] // parts)).reshape((-1,) + (1,) * (result.ndim - 1 - axis_at))

    near = jax.random.permutation(stream_key, parts)[block_of(target)]
    other_side = (block_of(target) + parts // 2) % parts
    return jnp.where((block_of(source) == near) | (block_of(source) == other_side), factor * result, result)


def shard_levels(own_key, extent, shards, least, largest):
    factor_of = 1.0
    for position, parts in shards:
        heights = jax.random.uniform(jax.random.fold_in(jax.random.fold_in(own_key, 6), position), (parts,), jnp.float32, least / len(shards), largest / len(shards))
        factor_of = factor_of * jnp.repeat(jnp.exp(heights), extent[position] // parts).reshape((-1,) + (1,) * (len(extent) - 1 - position))
    return factor_of


def centred(rng, extent, deviation, most, cuts=(), held_as=jnp.bfloat16):
    entries = deviation * jax.random.normal(rng, extent, jnp.float32)
    if cuts:
        entries = entries * shard_levels(rng, extent, cuts, -0.22, 0.18)
    return jnp.clip(entries, -most, most).astype(held_as)


def heavy_noise(key, shape, scale, limit, shards, heavy, kind=jnp.bfloat16):
    values = scale * jax.random.normal(key, shape, jnp.float32)
    if shards:
        values = values * shard_levels(key, shape, shards, -0.22, 0.18)
    return jnp.clip(spiked(values, jax.random.fold_in(key, 3), *heavy), -limit, limit).astype(kind)


def setup_inputs(seed: int = 0) -> dict:
    key_list = jax.random.split(jax.random.key(seed), 11)
    prefix_hidden = heavy_noise(key_list[0], (SAMPLES, PREFIX, D), 1.0, 6.0, ((0, 16), (1, 2)), (0, 2, 16, 2.0))
    norm_gain = jnp.clip(1.0 + 0.1 * jax.random.normal(key_list[1], (D,), jnp.float32), 0.5, 1.5)
    kv_weight = centred(key_list[2], (D, 2, KVH * HD), D ** -0.5, 0.0625, ((0, 8), (2, 2)))
    action_query = draw_action_query(jax.random.fold_in(key_list[10], 71), 0)
    action_kv = draw_action_kv(jax.random.fold_in(key_list[10], 71), 0)
    out_cotangent = centred(key_list[5], (SAMPLES, ACT, QH * HD), 3.0, 18.0, ((0, 16), (2, 2)))
    prefix_blocks = draw_prefix_blocks(jax.random.fold_in(key_list[10], 71), 0)
    action_blocks = draw_action_blocks(jax.random.fold_in(key_list[10], 71), 0)
    prefix_lengths = draw_prefix_lengths(jax.random.fold_in(key_list[10], 71), 0)
    timesteps = place_ends(jax.random.randint(key_list[9], (SAMPLES,), 0, STEPS), jax.random.fold_in(key_list[9], 1), 0, STEPS - 1).astype(jnp.int32)
    return dict(prefix_hidden=prefix_hidden, norm_gain=norm_gain, kv_weight=kv_weight, action_query=action_query, action_kv=action_kv, out_cotangent=out_cotangent, prefix_blocks=prefix_blocks, action_blocks=action_blocks, prefix_lengths=prefix_lengths, timesteps=timesteps)


EPS = 1e-06
NEGATIVE = -1e+30

def attention_pass(query, keys, values, visible, grad_out):
    scale = HD ** (-0.5)
    scores = jnp.einsum('agrh,jgh->graj', query.astype(jnp.float32), keys.astype(jnp.float32)) * scale
    masked = jnp.where(visible, scores, NEGATIVE)
    top = lax.optimization_barrier(jnp.max(masked, axis=-1, keepdims=True))
    expo = jnp.where(visible, jnp.exp(masked - top), 0.0)
    probs = expo / lax.optimization_barrier(jnp.sum(expo, axis=-1, keepdims=True))
    probs_low = lax.optimization_barrier(probs.astype(jnp.bfloat16)).astype(jnp.float32)
    out = jnp.einsum('graj,jgh->agrh', probs_low, values.astype(jnp.float32))
    d_probs = jnp.einsum('agrh,jgh->graj', grad_out.astype(jnp.float32), values.astype(jnp.float32))
    delta = lax.optimization_barrier(jnp.sum(probs * d_probs, axis=-1, keepdims=True))
    d_scores = lax.optimization_barrier((probs * (d_probs - delta)).astype(jnp.bfloat16)).astype(jnp.float32)
    d_query = jnp.einsum('graj,jgh->agrh', d_scores, keys.astype(jnp.float32)) * scale
    d_keys = jnp.einsum('graj,agrh->jgh', d_scores, query.astype(jnp.float32)) * scale
    d_values = jnp.einsum('graj,agrh->jgh', probs_low, grad_out.astype(jnp.float32))
    return (out, d_query, d_keys, d_values)

def reference(prefix_hidden, norm_gain, kv_weight, action_query, action_kv, out_cotangent, prefix_blocks, action_blocks, prefix_lengths, timesteps):
    ratio = QH // KVH
    columns = 2 * KVH * HD
    weight_flat = kv_weight.reshape(D, columns)
    positions = jnp.arange(PREFIX, dtype=jnp.int32)

    def one_sample(carry, inputs):
        hidden, query, own_pair, cotangent, pblocks, ablocks, length, level = inputs
        wide = hidden.astype(jnp.float32)
        inverse = lax.rsqrt(lax.optimization_barrier(jnp.mean(wide * wide, axis=-1, keepdims=True)) + EPS)
        normed = (wide * inverse * norm_gain).astype(jnp.bfloat16)
        prefix_kv = jnp.dot(normed, weight_flat, preferred_element_type=jnp.float32).astype(jnp.bfloat16)
        prefix_kv = prefix_kv.reshape(PREFIX, 2, KVH, HD)
        action_pair = own_pair.reshape(ACT, 2, KVH, HD)
        keys = jnp.concatenate([prefix_kv[:, 0], action_pair[:, 0]], axis=0)
        values = jnp.concatenate([prefix_kv[:, 1], action_pair[:, 1]], axis=0)
        see_prefix = (pblocks[None, :] <= ablocks[:, None]) & (positions[None, :] < length)
        see_action = ablocks[None, :] <= ablocks[:, None]
        visible = jnp.concatenate([see_prefix, see_action], axis=1)
        flow_weight = 0.5 + (level.astype(jnp.float32) + 0.5) / STEPS
        grad_out = (flow_weight * cotangent.astype(jnp.float32)).astype(jnp.bfloat16).reshape(ACT, KVH, ratio, HD)
        out, d_query, d_keys, d_values = attention_pass(query.reshape(ACT, KVH, ratio, HD), keys, values, visible, grad_out)
        d_pair = jnp.stack([d_keys, d_values], axis=1)
        prefix_grad = d_pair[:PREFIX].astype(jnp.bfloat16).reshape(PREFIX, columns)
        term = jnp.dot(normed.T, prefix_grad, preferred_element_type=jnp.float32)
        carry = carry + lax.optimization_barrier(term.astype(jnp.bfloat16)).astype(jnp.float32)
        results = (out.astype(jnp.bfloat16).reshape(ACT, QH * HD), d_query.reshape(ACT, QH * HD), d_pair[PREFIX:].reshape(ACT, 2, KVH * HD))
        return (carry, results)
    start = jnp.zeros((D, columns), jnp.float32)
    total, outputs = lax.scan(one_sample, start, (prefix_hidden, action_query, action_kv, out_cotangent, prefix_blocks, action_blocks, prefix_lengths, timesteps))
    attn_out, query_grad, action_kv_grad = outputs
    return (attn_out, query_grad, action_kv_grad, total.reshape(D, 2, KVH * HD))
```

```python
import functools

import jax
import jax.numpy as jnp
from jax import lax
from jax.experimental import pallas as pl
from jax.experimental.pallas import tpu as pltpu
from jax.sharding import PartitionSpec as P

KVH = 8
HD = 128
QH = 16
STEPS = 1000


EPS = 1e-06
NEGATIVE = -1e30
CHUNKS = 4
MiB = 1 << 20


def inner_of(ndp):
    return 2 if ndp % 2 == 0 else 1


def remote(src, dst, send_sem, recv_sem, where):
    return pltpu.make_async_remote_copy(
        src_ref=src,
        dst_ref=dst,
        send_sem=send_sem,
        recv_sem=recv_sem,
        device_id=where,
        device_id_type=pl.DeviceIdType.MESH,
    )


def greet(peers):
    barrier = pltpu.get_barrier_semaphore()
    for peer in peers:
        pl.semaphore_signal(
            barrier, inc=1, device_id=peer, device_id_type=pl.DeviceIdType.MESH
        )
    pl.semaphore_wait(barrier, len(peers))


def gather_kernel(
    ndp, nmp, w_ref, n_ref, w_all, n_all,
    own_sem, zs, zr, xs, xr, ys, yr, ms, mr, fs, fr,
):
    nx = inner_of(ndp)
    nz = ndp // nx
    dp, seg, mp = lax.axis_index("dp"), lax.axis_index("segment"), lax.axis_index("mp")
    z, x = dp // nx, dp % nx
    z_peer = [{"dp": ((z + o) % nz) * nx + x} for o in range(1, nz)]
    x_peer = {"dp": z * nx + (nx - 1 - x)}
    y_peer = {"segment": 1 - seg}
    m_peer = [{"mp": (mp + o) % nmp} for o in range(1, nmp)]
    greet(z_peer + ([x_peer] if nx > 1 else []) + [y_peer] + m_peer)
    rows = n_ref.shape[0] // CHUNKS

    own_w = pltpu.make_async_copy(w_ref, w_all.at[dp], own_sem.at[0])
    own_n = pltpu.make_async_copy(n_ref, n_all.at[seg, mp], own_sem.at[1])
    started = []
    order = sorted(range(1, nz), key=lambda o: min(o, nz - o))
    z_copy = {o: remote(w_ref, w_all.at[dp], zs.at[o - 1], zr.at[o - 1], z_peer[o - 1]) for o in order}
    y_copy = [
        remote(
            n_ref.at[pl.ds(c * rows, rows)],
            n_all.at[seg, mp, pl.ds(c * rows, rows)],
            ys.at[c], yr.at[c], y_peer,
        )
        for c in range(CHUNKS)
    ]
    x_copy = []
    if nx > 1:
        x_copy.append(remote(w_ref, w_all.at[dp], xs.at[0], xr.at[0], x_peer))
    m_copy = [remote(n_ref, n_all.at[seg, mp], ms.at[o], mr.at[o], m_peer[o]) for o in range(nmp - 1)]
    for copy in list(z_copy.values()) + x_copy + y_copy + m_copy + [own_w, own_n]:
        copy.start()
    f_copy = []

    def on_z(o):
        z_copy[o].wait_recv()
        if nx > 1:
            src = ((z + nz - o) % nz) * nx + x
            copy = remote(w_all.at[src], w_all.at[src], xs.at[o], xr.at[o], x_peer)
            copy.start()
            x_copy.append(copy)

    def on_y(c):
        y_copy[c].wait_recv()
        for o in range(nmp - 1):
            part = n_all.at[1 - seg, mp, pl.ds(c * rows, rows)]
            copy = remote(part, part, fs.at[o, c], fr.at[o, c], m_peer[o])
            copy.start()
            f_copy.append(copy)

    for i in range(max(len(order), CHUNKS)):
        if i < len(order):
            on_z(order[i])
        if i < CHUNKS:
            on_y(i)
    own_w.wait()
    own_n.wait()
    for copy in m_copy + x_copy + f_copy:
        copy.wait_recv()
    for copy in list(z_copy.values()) + y_copy + m_copy + x_copy + f_copy:
        copy.wait_send()


def gather(ndp, nseg, nmp, weight, normed):
    nx = inner_of(ndp)
    nz = ndp // nx
    dma = pltpu.SemaphoreType.DMA
    vmem = pl.BlockSpec(memory_space=pltpu.VMEM)
    anys = pl.BlockSpec(memory_space=pl.ANY)
    return pl.pallas_call(
        functools.partial(gather_kernel, ndp, nmp),
        out_shape=(
            jax.ShapeDtypeStruct((ndp,) + weight.shape, weight.dtype),
            jax.ShapeDtypeStruct((nseg, nmp) + normed.shape, normed.dtype),
        ),
        in_specs=[vmem, vmem],
        out_specs=(anys, anys),
        scratch_shapes=[
            dma((2,)),
            dma((max(nz - 1, 1),)), dma((max(nz - 1, 1),)),
            dma((nz,)), dma((nz,)),
            dma((CHUNKS,)), dma((CHUNKS,)),
            dma((max(nmp - 1, 1),)), dma((max(nmp - 1, 1),)),
            dma((max(nmp - 1, 1), CHUNKS)), dma((max(nmp - 1, 1), CHUNKS)),
        ],
        compiler_params=pltpu.CompilerParams(
            collective_id=0, has_side_effects=True, vmem_limit_bytes=16 * MiB
        ),
        name="gather",
    )(weight, normed)


def attention_kernel(
    heads, ratio, kvc, q_ref, akv_ref, go_ref, vis_ref,
    out_ref, dq_ref, dakv_ref, g_ref, pair, grad, sems,
):
    seg = lax.axis_index("segment")
    peer = {"segment": 1 - seg}
    greet([peer])
    give = remote(kvc.at[1 - seg], pair.at[seg], sems.at[0], sems.at[1], peer)
    give.start()
    keep = pltpu.make_async_copy(kvc.at[seg], pair.at[seg], sems.at[2])
    keep.start()
    keep.wait()
    give.wait()
    acts = q_ref.shape[0]
    rows = pair.shape[1]
    scale = HD ** (-0.5)
    vis = vis_ref[...]
    visible = jnp.concatenate([vis] * ratio, axis=0) > 0.5

    def dot(a, b, ca, cb):
        return lax.dot_general(a, b, (((ca,), (cb,)), ((), ())), preferred_element_type=jnp.float32)

    for g in range(heads):
        cols = slice(g * HD, (g + 1) * HD)
        keys = jnp.concatenate([pair[0, :, cols], akv_ref[0, :, cols]], axis=0)
        values = jnp.concatenate([pair[1, :, cols], akv_ref[1, :, cols]], axis=0)
        hs = [slice((g * ratio + r) * HD, (g * ratio + r + 1) * HD) for r in range(ratio)]
        query = jnp.concatenate([q_ref[:, h] for h in hs], axis=0)
        go = jnp.concatenate([go_ref[:, h] for h in hs], axis=0)
        masked = jnp.where(visible, dot(query, keys, 1, 1) * scale, NEGATIVE)
        top = jnp.max(masked, axis=-1, keepdims=True)
        expo = jnp.where(visible, jnp.exp(masked - top), 0.0)
        probs = expo * (1.0 / jnp.sum(expo, axis=-1, keepdims=True))
        low = probs.astype(jnp.bfloat16)
        d_probs = dot(go, values, 1, 1)
        delta = jnp.sum(probs * d_probs, axis=-1, keepdims=True)
        d_scores = (probs * (d_probs - delta)).astype(jnp.bfloat16)
        out = dot(low, values, 1, 0).astype(jnp.bfloat16)
        d_query = dot(d_scores, keys, 1, 0) * scale
        for r, h in enumerate(hs):
            out_ref[:, h] = out[r * acts : (r + 1) * acts]
            dq_ref[:, h] = d_query[r * acts : (r + 1) * acts]
        d_keys = dot(d_scores, query, 0, 0) * scale
        d_values = dot(low, go, 0, 0)
        grad[0, :, cols] = d_keys[:rows].astype(jnp.bfloat16)
        grad[1, :, cols] = d_values[:rows].astype(jnp.bfloat16)
        dakv_ref[0, :, cols] = d_keys[rows:]
        dakv_ref[1, :, cols] = d_values[rows:]
    back = remote(grad.at[1 - seg], g_ref.at[seg], sems.at[3], sems.at[4], peer)
    back.start()
    local = pltpu.make_async_copy(grad.at[seg], g_ref.at[seg], sems.at[5])
    local.start()
    local.wait()
    back.wait()


def attention(heads, ratio, kvc, query, akv, grad_out, visible):
    vmem = pl.BlockSpec(memory_space=pltpu.VMEM)
    acts, width = query.shape
    return pl.pallas_call(
        functools.partial(attention_kernel, heads, ratio),
        out_shape=(
            jax.ShapeDtypeStruct((acts, width), jnp.bfloat16),
            jax.ShapeDtypeStruct((acts, width), jnp.float32),
            jax.ShapeDtypeStruct(akv.shape, jnp.float32),
            jax.ShapeDtypeStruct(kvc.shape, jnp.bfloat16),
        ),
        in_specs=[vmem] * 5,
        out_specs=(vmem,) * 4,
        scratch_shapes=[
            pltpu.VMEM(kvc.shape, jnp.bfloat16),
            pltpu.VMEM(kvc.shape, jnp.bfloat16),
            pltpu.SemaphoreType.DMA((6,)),
        ],
        compiler_params=pltpu.CompilerParams(
            collective_id=1, has_side_effects=True, vmem_limit_bytes=32 * MiB
        ),
        name="attention",
    )(kvc, query, akv, grad_out, visible)


def scatter_kernel(ndp, t_ref, o_ref, x_buf, z_send, z_buf, xs, xr, zs, zr, ys):
    nx = inner_of(ndp)
    nz = ndp // nx
    dp, seg = lax.axis_index("dp"), lax.axis_index("segment")
    z, x = dp // nx, dp % nx
    z_peer = [{"dp": ((z + o) % nz) * nx + x} for o in range(1, nz)]
    x_peer = {"dp": z * nx + (nx - 1 - x)}
    y_peer = {"segment": 1 - seg}
    greet(z_peer + ([x_peer] if nx > 1 else []) + [y_peer])
    order = sorted(range(1, nz), key=lambda o: -min(o, nz - o)) + [0]
    rows = t_ref.shape[1]
    step = min(rows, 64)
    x_copy = {}
    if nx > 1:
        for o in order:
            block = ((z + o) % nz) * nx + (nx - 1 - x)
            x_copy[o] = remote(t_ref.at[block], x_buf.at[o], xs.at[o], xr.at[o], x_peer)
            x_copy[o].start()
    z_copy = {}
    for o in order:
        block = ((z + o) % nz) * nx + x
        if nx > 1:
            x_copy[o].wait_recv()

        @pl.loop(0, rows // step)
        def _(i):
            part = pl.ds(pl.multiple_of(i * step, step), step)
            total = t_ref[block, part, :].astype(jnp.float32)
            if nx > 1:
                total = total + x_buf[o, part, :].astype(jnp.float32)
            z_send[o, part, :] = total.astype(jnp.bfloat16)

        if o > 0:
            z_copy[o] = remote(z_send.at[o], z_buf.at[o], zs.at[o], zr.at[o], z_peer[o - 1])
            z_copy[o].start()
    for copy in z_copy.values():
        copy.wait_recv()

    @pl.loop(0, rows // step)
    def _(i):
        part = pl.ds(pl.multiple_of(i * step, step), step)
        total = z_send[0, part, :].astype(jnp.float32)
        for o in range(1, nz):
            total = total + z_buf[o, part, :].astype(jnp.float32)
        z_buf[0, part, :] = total.astype(jnp.bfloat16)

    last = remote(z_buf.at[0], o_ref.at[seg], ys.at[0], ys.at[1], y_peer)
    last.start()
    local = pltpu.make_async_copy(z_buf.at[0], o_ref.at[seg], ys.at[2])
    local.start()
    local.wait()
    last.wait()
    for copy in list(x_copy.values()) + list(z_copy.values()):
        copy.wait_send()


def scatter(ndp, nseg, term):
    nx = inner_of(ndp)
    nz = ndp // nx
    dma = pltpu.SemaphoreType.DMA
    vmem = pl.BlockSpec(memory_space=pltpu.VMEM)
    block = term.shape[1:]
    return pl.pallas_call(
        functools.partial(scatter_kernel, ndp),
        out_shape=jax.ShapeDtypeStruct((nseg,) + block, jnp.bfloat16),
        in_specs=[vmem],
        out_specs=vmem,
        scratch_shapes=[pltpu.VMEM((nz,) + block, jnp.bfloat16)] * 3 + [dma((nz,))] * 4 + [dma((3,))],
        compiler_params=pltpu.CompilerParams(
            collective_id=2, has_side_effects=True, vmem_limit_bytes=40 * MiB
        ),
        name="scatter",
    )(term)


def shards(
    ndp,
    nseg,
    nmp,
    prefix_hidden,
    norm_gain,
    kv_weight,
    action_query,
    action_kv,
    out_cotangent,
    prefix_blocks,
    action_blocks,
    prefix_lengths,
    timesteps,
):
    heads_kv = kv_weight.shape[2] // HD
    ratio = QH // KVH
    columns = kv_weight.shape[2]
    seg = lax.axis_index("segment")
    wide = prefix_hidden[0].astype(jnp.float32)
    inverse = lax.rsqrt(jnp.mean(wide * wide, axis=-1, keepdims=True) + EPS)
    normed_local = (wide * inverse * norm_gain).astype(jnp.bfloat16)
    own_weight = lax.dynamic_index_in_dim(kv_weight, seg, axis=1, keepdims=False)
    weights, normed = gather(ndp, nseg, nmp, own_weight, normed_local)
    rows = nmp * normed_local.shape[0]
    width = normed_local.shape[1]
    tokens = normed.reshape(nseg * rows, width)
    projected = jnp.dot(
        tokens, weights.reshape(width, columns), preferred_element_type=jnp.float32
    )
    kvc = projected.astype(jnp.bfloat16).reshape(nseg, rows, columns)
    flow_weight = 0.5 + (timesteps[0].astype(jnp.float32) + 0.5) / STEPS
    grad_out = (flow_weight * out_cotangent[0].astype(jnp.float32)).astype(jnp.bfloat16)
    pblocks = prefix_blocks[0]
    ablocks = action_blocks[0]
    positions = jnp.arange(rows, dtype=jnp.int32)
    see_prefix = (pblocks[None, :] <= ablocks[:, None]) & (positions[None, :] < prefix_lengths[0])
    see_action = ablocks[None, :] <= ablocks[:, None]
    visible = jnp.concatenate([see_prefix, see_action], axis=1).astype(jnp.float32)
    attn_out, query_grad, d_action, grads = attention(
        heads_kv, ratio, kvc, action_query[0], action_kv[0].transpose(1, 0, 2), grad_out, visible
    )
    term = lax.dot_general(
        tokens,
        grads.reshape(nseg * rows, columns),
        (((0,), (0,)), ((), ())),
        preferred_element_type=jnp.float32,
    ).astype(jnp.bfloat16)
    summed = scatter(ndp, nseg, term.reshape(ndp, width // ndp, columns))
    weight_grad = summed.transpose(1, 0, 2).astype(jnp.float32)
    return (attn_out[None], query_grad[None], d_action.transpose(1, 0, 2)[None], weight_grad)


def solution(mesh):
    placed = (
        P(("dp", "segment"), "mp", None),
        P(),
        P("dp", None, "mp"),
        P(("dp", "segment"), None, "mp"),
        P(("dp", "segment"), None, None, "mp"),
        P(("dp", "segment"), None, "mp"),
        P(("dp", "segment"), None),
        P(("dp", "segment"), None),
        P(("dp", "segment")),
        P(("dp", "segment")),
    )
    return jax.shard_map(
        functools.partial(shards, mesh.shape["dp"], mesh.shape["segment"], mesh.shape["mp"]),
        mesh=mesh,
        in_specs=placed,
        out_specs=(
            P(("dp", "segment"), None, "mp"),
            P(("dp", "segment"), None, "mp"),
            P(("dp", "segment"), None, None, "mp"),
            P("dp", None, "mp"),
        ),
        check_vma=False,
    )
```

```python
import functools

import jax
import jax.numpy as jnp
from jax import lax
from jax.experimental import pallas as pl
from jax.experimental.pallas import tpu as pltpu
from jax.sharding import PartitionSpec as P

KVH = 8
HD = 128
QH = 16
STEPS = 1000


EPS = 1e-06
NEGATIVE = -1e30
CHUNKS = 4
MiB = 1 << 20


def inner_of(ndp):
    return 2 if ndp % 2 == 0 else 1


def remote(src, dst, send_sem, recv_sem, where):
    return pltpu.make_async_remote_copy(
        src_ref=src,
        dst_ref=dst,
        send_sem=send_sem,
        recv_sem=recv_sem,
        device_id=where,
        device_id_type=pl.DeviceIdType.MESH,
    )


def greet(peers):
    barrier = pltpu.get_barrier_semaphore()
    for peer in peers:
        pl.semaphore_signal(
            barrier, inc=1, device_id=peer, device_id_type=pl.DeviceIdType.MESH
        )
    pl.semaphore_wait(barrier, len(peers))


def project_kernel(
    ndp, nmp, w_ref, n_ref, kvc_ref, n_all, w_all, acc,
    own_sem, zs, zr, xs, xr, ys, yr, ms, mr, fs, fr,
):
    nx = inner_of(ndp)
    nz = ndp // nx
    dp, seg, mp = lax.axis_index("dp"), lax.axis_index("segment"), lax.axis_index("mp")
    z, x = dp // nx, dp % nx
    z_peer = [{"dp": ((z + o) % nz) * nx + x} for o in range(1, nz)]
    x_peer = {"dp": z * nx + (nx - 1 - x)}
    y_peer = {"segment": 1 - seg}
    m_peer = [{"mp": (mp + o) % nmp} for o in range(1, nmp)]
    greet(z_peer + ([x_peer] if nx > 1 else []) + [y_peer] + m_peer)
    depth = w_ref.shape[0]
    step = depth // CHUNKS
    mine, theirs = seg * nmp + mp, (1 - seg) * nmp + mp
    order = [0] + sorted(range(1, nz), key=lambda o: min(o, nz - o))

    def outer(o):
        return (z + nz - o) % nz

    def columns(o):
        return pl.ds(pl.multiple_of(outer(o) * (nx * depth), nx * depth), nx * depth)

    def z_copy(o, c):
        part = pl.ds(c * step, step)
        return remote(w_ref.at[part], w_all.at[dp, part], zs.at[o - 1, c], zr.at[o - 1, c], z_peer[o - 1])

    def x_copy(o, c):
        part = pl.ds(c * step, step)
        src = outer(o) * nx + x
        held = w_ref.at[part] if o == 0 else w_all.at[src, part]
        return remote(held, w_all.at[src, part], xs.at[o, c], xr.at[o, c], x_peer)

    def y_copy(o):
        return remote(n_ref.at[:, columns(o)], n_all.at[mine, :, columns(o)], ys.at[o], yr.at[o], y_peer)

    def m_copy(p):
        return remote(n_ref, n_all.at[mine], ms.at[p], mr.at[p], m_peer[p])

    def f_copy(o, p):
        part = n_all.at[theirs, :, columns(o)]
        return remote(part, part, fs.at[o, p], fr.at[o, p], m_peer[p])

    own_w = pltpu.make_async_copy(w_ref, w_all.at[dp], own_sem.at[0])
    own_n = pltpu.make_async_copy(n_ref, n_all.at[mine], own_sem.at[1])
    for o in order[1:]:
        for c in range(CHUNKS):
            z_copy(o, c).start()
    if nx > 1:
        for c in range(CHUNKS):
            x_copy(0, c).start()
    for o in order:
        y_copy(o).start()
    for p in range(nmp - 1):
        m_copy(p).start()
    own_w.start()
    own_n.start()
    acc[...] = jnp.zeros_like(acc)

    def multiply(block):
        cols = pl.ds(pl.multiple_of(block * depth, depth), depth)

        @pl.loop(0, n_all.shape[0])
        def _(i):
            acc[i] += jnp.dot(n_all[i, :, cols], w_all[block], preferred_element_type=jnp.float32)

    def finish(o):
        for p in range(nmp - 1):
            f_copy(o, p).wait_recv()
        if o == 0:
            own_w.wait()
            own_n.wait()
            for p in range(nmp - 1):
                m_copy(p).wait_recv()
        multiply(outer(o) * nx + x)
        if nx > 1:
            for c in range(CHUNKS):
                x_copy(o, c).wait_recv()
            multiply(outer(o) * nx + (nx - 1 - x))

    for i, o in enumerate(order):
        if o > 0:
            for c in range(CHUNKS):
                z_copy(o, c).wait_recv()
                if nx > 1:
                    x_copy(o, c).start()
        y_copy(o).wait_recv()
        for p in range(nmp - 1):
            f_copy(o, p).start()
        if i > 0:
            finish(order[i - 1])
    finish(order[-1])
    kvc_ref[...] = acc[...].astype(kvc_ref.dtype)
    for o in order:
        if o > 0:
            for c in range(CHUNKS):
                z_copy(o, c).wait_send()
        if nx > 1:
            for c in range(CHUNKS):
                x_copy(o, c).wait_send()
        y_copy(o).wait_send()
        for p in range(nmp - 1):
            f_copy(o, p).wait_send()
    for p in range(nmp - 1):
        m_copy(p).wait_send()


def project(ndp, nseg, nmp, weight, normed):
    nx = inner_of(ndp)
    nz = ndp // nx
    dma = pltpu.SemaphoreType.DMA
    vmem = pl.BlockSpec(memory_space=pltpu.VMEM)
    rows, width = normed.shape
    cols = weight.shape[1]
    others, further = max(nmp - 1, 1), max(nz - 1, 1)
    return pl.pallas_call(
        functools.partial(project_kernel, ndp, nmp),
        out_shape=(
            jax.ShapeDtypeStruct((nseg * nmp, rows, cols), jnp.bfloat16),
            jax.ShapeDtypeStruct((nseg * nmp, rows, width), normed.dtype),
        ),
        in_specs=[vmem, vmem],
        out_specs=(vmem, vmem),
        scratch_shapes=[
            pltpu.VMEM((ndp,) + weight.shape, weight.dtype),
            pltpu.VMEM((nseg * nmp, rows, cols), jnp.float32),
            dma((2,)),
            dma((further, CHUNKS)), dma((further, CHUNKS)),
            dma((nz, CHUNKS)), dma((nz, CHUNKS)),
            dma((nz,)), dma((nz,)),
            dma((others,)), dma((others,)),
            dma((nz, others)), dma((nz, others)),
        ],
        compiler_params=pltpu.CompilerParams(
            collective_id=0, has_side_effects=True, vmem_limit_bytes=20 * MiB
        ),
        name="project",
    )(weight, normed)


def attention_kernel(
    heads, ratio, kvc, q_ref, akv_ref, go_ref, vis_ref,
    out_ref, dq_ref, dakv_ref, g_ref, pair, grad, sems,
):
    seg = lax.axis_index("segment")
    peer = {"segment": 1 - seg}
    greet([peer])
    give = remote(kvc.at[1 - seg], pair.at[seg], sems.at[0], sems.at[1], peer)
    give.start()
    keep = pltpu.make_async_copy(kvc.at[seg], pair.at[seg], sems.at[2])
    keep.start()
    keep.wait()
    give.wait()
    acts = q_ref.shape[0]
    rows = pair.shape[1]
    scale = HD ** (-0.5)
    vis = vis_ref[...]
    visible = jnp.concatenate([vis] * ratio, axis=0) > 0.5

    def dot(a, b, ca, cb):
        return lax.dot_general(a, b, (((ca,), (cb,)), ((), ())), preferred_element_type=jnp.float32)

    for g in range(heads):
        cols = slice(g * HD, (g + 1) * HD)
        keys = jnp.concatenate([pair[0, :, cols], akv_ref[0, :, cols]], axis=0)
        values = jnp.concatenate([pair[1, :, cols], akv_ref[1, :, cols]], axis=0)
        hs = [slice((g * ratio + r) * HD, (g * ratio + r + 1) * HD) for r in range(ratio)]
        query = jnp.concatenate([q_ref[:, h] for h in hs], axis=0)
        go = jnp.concatenate([go_ref[:, h] for h in hs], axis=0)
        masked = jnp.where(visible, dot(query, keys, 1, 1) * scale, NEGATIVE)
        top = jnp.max(masked, axis=-1, keepdims=True)
        expo = jnp.where(visible, jnp.exp(masked - top), 0.0)
        probs = expo * (1.0 / jnp.sum(expo, axis=-1, keepdims=True))
        low = probs.astype(jnp.bfloat16)
        d_probs = dot(go, values, 1, 1)
        delta = jnp.sum(probs * d_probs, axis=-1, keepdims=True)
        d_scores = (probs * (d_probs - delta)).astype(jnp.bfloat16)
        out = dot(low, values, 1, 0).astype(jnp.bfloat16)
        d_query = dot(d_scores, keys, 1, 0) * scale
        for r, h in enumerate(hs):
            out_ref[:, h] = out[r * acts : (r + 1) * acts]
            dq_ref[:, h] = d_query[r * acts : (r + 1) * acts]
        d_keys = dot(d_scores, query, 0, 0) * scale
        d_values = dot(low, go, 0, 0)
        grad[0, :, cols] = d_keys[:rows].astype(jnp.bfloat16)
        grad[1, :, cols] = d_values[:rows].astype(jnp.bfloat16)
        dakv_ref[0, :, cols] = d_keys[rows:]
        dakv_ref[1, :, cols] = d_values[rows:]
    back = remote(grad.at[1 - seg], g_ref.at[seg], sems.at[3], sems.at[4], peer)
    back.start()
    local = pltpu.make_async_copy(grad.at[seg], g_ref.at[seg], sems.at[5])
    local.start()
    local.wait()
    back.wait()


def attention(heads, ratio, kvc, query, akv, grad_out, visible):
    vmem = pl.BlockSpec(memory_space=pltpu.VMEM)
    acts, width = query.shape
    return pl.pallas_call(
        functools.partial(attention_kernel, heads, ratio),
        out_shape=(
            jax.ShapeDtypeStruct((acts, width), jnp.bfloat16),
            jax.ShapeDtypeStruct((acts, width), jnp.float32),
            jax.ShapeDtypeStruct(akv.shape, jnp.float32),
            jax.ShapeDtypeStruct(kvc.shape, jnp.bfloat16),
        ),
        in_specs=[vmem] * 5,
        out_specs=(vmem,) * 4,
        scratch_shapes=[
            pltpu.VMEM(kvc.shape, jnp.bfloat16),
            pltpu.VMEM(kvc.shape, jnp.bfloat16),
            pltpu.SemaphoreType.DMA((6,)),
        ],
        compiler_params=pltpu.CompilerParams(
            collective_id=1, has_side_effects=True, vmem_limit_bytes=12 * MiB
        ),
        name="attention",
    )(kvc, query, akv, grad_out, visible)


def scatter_kernel(ndp, n_ref, g_ref, o_ref, x_send, x_buf, z_send, z_buf, xs, xr, zs, zr, ys, yr):
    nx = inner_of(ndp)
    nz = ndp // nx
    dp, seg = lax.axis_index("dp"), lax.axis_index("segment")
    z, x = dp // nx, dp % nx
    z_peer = [{"dp": ((z + o) % nz) * nx + x} for o in range(1, nz)]
    x_peer = {"dp": z * nx + (nx - 1 - x)}
    y_peer = {"segment": 1 - seg}
    greet(z_peer + ([x_peer] if nx > 1 else []) + [y_peer])
    order = sorted(range(1, nz), key=lambda o: -min(o, nz - o)) + [0]
    rows = o_ref.shape[1]
    step = min(rows, max(rows // CHUNKS, 128))
    steps = rows // step

    def part(c):
        return pl.ds(pl.multiple_of(c * step, step), step)

    def term(block, c):
        cols = pl.ds(pl.multiple_of(block * rows + c * step, step), step)
        return lax.dot_general(
            n_ref[:, cols], g_ref[...], (((0,), (0,)), ((), ())), preferred_element_type=jnp.float32
        )

    def x_copy(o, c):
        return remote(x_send.at[o, part(c)], x_buf.at[o, part(c)], xs.at[o, c], xr.at[o, c], x_peer)

    def z_copy(o, c):
        return remote(z_send.at[o, part(c)], z_buf.at[o, part(c)], zs.at[o, c], zr.at[o, c], z_peer[o - 1])

    def y_copy(c):
        return remote(o_ref.at[seg, part(c)], o_ref.at[seg, part(c)], ys.at[c], yr.at[c], y_peer)

    if nx > 1:
        for o in order:
            @pl.loop(0, steps)
            def _(c):
                x_send[o, part(c), :] = term(((z + o) % nz) * nx + (nx - 1 - x), c).astype(jnp.bfloat16)
                x_copy(o, c).start()

    for o in order:
        @pl.loop(0, steps)
        def _(c):
            total = term(((z + o) % nz) * nx + x, c)
            if nx > 1:
                x_copy(o, c).wait_recv()
                total = total + x_buf[o, part(c), :].astype(jnp.float32)
            if o > 0:
                z_send[o, part(c), :] = total.astype(jnp.bfloat16)
                z_copy(o, c).start()
            else:
                for other in order[:-1]:
                    z_copy(other, c).wait_recv()
                    total = total + z_buf[other, part(c), :].astype(jnp.float32)
                o_ref[seg, part(c), :] = total.astype(jnp.bfloat16)
                y_copy(c).start()

    @pl.loop(0, steps)
    def _(c):
        y_copy(c).wait()
        for o in order:
            if nx > 1:
                x_copy(o, c).wait_send()
            if o > 0:
                z_copy(o, c).wait_send()


def scatter(ndp, nseg, tokens, grads):
    nx = inner_of(ndp)
    nz = ndp // nx
    dma = pltpu.SemaphoreType.DMA
    vmem = pl.BlockSpec(memory_space=pltpu.VMEM)
    block = (tokens.shape[1] // ndp, grads.shape[1])
    return pl.pallas_call(
        functools.partial(scatter_kernel, ndp),
        out_shape=jax.ShapeDtypeStruct((nseg,) + block, jnp.bfloat16),
        in_specs=[vmem, vmem],
        out_specs=vmem,
        scratch_shapes=[pltpu.VMEM((nz,) + block, jnp.bfloat16)] * 4
        + [dma((nz, CHUNKS))] * 4
        + [dma((CHUNKS,))] * 2,
        compiler_params=pltpu.CompilerParams(
            collective_id=2, has_side_effects=True, vmem_limit_bytes=24 * MiB
        ),
        name="scatter",
    )(tokens, grads)


def shards(
    ndp,
    nseg,
    nmp,
    prefix_hidden,
    norm_gain,
    kv_weight,
    action_query,
    action_kv,
    out_cotangent,
    prefix_blocks,
    action_blocks,
    prefix_lengths,
    timesteps,
):
    heads_kv = kv_weight.shape[2] // HD
    ratio = QH // KVH
    columns = kv_weight.shape[2]
    seg = lax.axis_index("segment")
    wide = prefix_hidden[0].astype(jnp.float32)
    inverse = lax.rsqrt(jnp.mean(wide * wide, axis=-1, keepdims=True) + EPS)
    normed_local = (wide * inverse * norm_gain).astype(jnp.bfloat16)
    own_weight = lax.dynamic_index_in_dim(kv_weight, seg, axis=1, keepdims=False)
    kvc, tokens = project(ndp, nseg, nmp, own_weight, normed_local)
    rows = nmp * normed_local.shape[0]
    width = normed_local.shape[1]
    kvc = kvc.reshape(nseg, rows, columns)
    flow_weight = 0.5 + (timesteps[0].astype(jnp.float32) + 0.5) / STEPS
    grad_out = (flow_weight * out_cotangent[0].astype(jnp.float32)).astype(jnp.bfloat16)
    pblocks = prefix_blocks[0]
    ablocks = action_blocks[0]
    positions = jnp.arange(rows, dtype=jnp.int32)
    see_prefix = (pblocks[None, :] <= ablocks[:, None]) & (positions[None, :] < prefix_lengths[0])
    see_action = ablocks[None, :] <= ablocks[:, None]
    visible = jnp.concatenate([see_prefix, see_action], axis=1).astype(jnp.float32)
    attn_out, query_grad, d_action, grads = attention(
        heads_kv, ratio, kvc, action_query[0], action_kv[0].transpose(1, 0, 2), grad_out, visible
    )
    summed = scatter(
        ndp, nseg, tokens.reshape(nseg * rows, width), grads.reshape(nseg * rows, columns)
    )
    weight_grad = summed.transpose(1, 0, 2).astype(jnp.float32)
    return (attn_out[None], query_grad[None], d_action.transpose(1, 0, 2)[None], weight_grad)


def solution(mesh):
    placed = (
        P(("dp", "segment"), "mp", None),
        P(),
        P("dp", None, "mp"),
        P(("dp", "segment"), None, "mp"),
        P(("dp", "segment"), None, None, "mp"),
        P(("dp", "segment"), None, "mp"),
        P(("dp", "segment"), None),
        P(("dp", "segment"), None),
        P(("dp", "segment")),
        P(("dp", "segment")),
    )
    return jax.shard_map(
        functools.partial(shards, mesh.shape["dp"], mesh.shape["segment"], mesh.shape["mp"]),
        mesh=mesh,
        in_specs=placed,
        out_specs=(
            P(("dp", "segment"), None, "mp"),
            P(("dp", "segment"), None, "mp"),
            P(("dp", "segment"), None, None, "mp"),
            P("dp", None, "mp"),
        ),
        check_vma=False,
    )
```

```python
import functools

import jax
import jax.numpy as jnp
from jax import lax
from jax.experimental import pallas as pl
from jax.experimental.pallas import tpu as pltpu
from jax.sharding import PartitionSpec as P

KVH = 8
HD = 128
QH = 16
STEPS = 1000


EPS = 1e-06
NEGATIVE = -1e30
CHUNKS = 4
MiB = 1 << 20


def inner_of(ndp):
    return 2 if ndp % 2 == 0 else 1


def remote(src, dst, send_sem, recv_sem, where):
    return pltpu.make_async_remote_copy(
        src_ref=src,
        dst_ref=dst,
        send_sem=send_sem,
        recv_sem=recv_sem,
        device_id=where,
        device_id_type=pl.DeviceIdType.MESH,
    )


def greet(peers):
    barrier = pltpu.get_barrier_semaphore()
    for peer in peers:
        pl.semaphore_signal(
            barrier, inc=1, device_id=peer, device_id_type=pl.DeviceIdType.MESH
        )
    pl.semaphore_wait(barrier, len(peers))


def project_kernel(
    ndp, nmp, w_ref, n_ref, kvc_ref, n_all, w_all, acc,
    own_sem, zs, zr, xs, xr, ys, yr, ms, mr, fs, fr,
):
    nx = inner_of(ndp)
    nz = ndp // nx
    dp, seg, mp = lax.axis_index("dp"), lax.axis_index("segment"), lax.axis_index("mp")
    z, x = dp // nx, dp % nx
    up, down = {"dp": ((z + 1) % nz) * nx + x}, {"dp": ((z + nz - 1) % nz) * nx + x}
    x_peer = {"dp": z * nx + (nx - 1 - x)}
    y_peer = {"segment": 1 - seg}
    m_peer = [{"mp": (mp + o) % nmp} for o in range(1, nmp)]
    near = [up, down] if nz > 2 else [up] if nz > 1 else []
    greet(near + ([x_peer] if nx > 1 else []) + [y_peer] + m_peer)
    depth = w_ref.shape[0]
    step = depth // CHUNKS
    mine, theirs = seg * nmp + mp, (1 - seg) * nmp + mp

    def columns(src):
        return pl.ds(pl.multiple_of(src * (nx * depth), nx * depth), nx * depth)

    def part(c):
        return pl.ds(pl.multiple_of(c * step, step), step)

    def hop(src, c, rising):
        held = w_all.at[src * nx + x, part(c)]
        side = 0 if rising else 1
        return remote(held, held, zs.at[side, src, c], zr.at[src, c], up if rising else down)

    def x_copy(src, c):
        held = w_all.at[src * nx + x, part(c)]
        return remote(held, held, xs.at[src, c], xr.at[src, c], x_peer)

    def y_copy(src):
        return remote(n_ref.at[:, columns(src)], n_all.at[mine, :, columns(src)], ys.at[src], yr.at[src], y_peer)

    def m_copy(p):
        return remote(n_ref, n_all.at[mine], ms.at[p], mr.at[p], m_peer[p])

    def f_copy(src, p):
        held = n_all.at[theirs, :, columns(src)]
        return remote(held, held, fs.at[src, p], fr.at[src, p], m_peer[p])

    def at_level(level, act):
        @pl.when(z - level >= 0)
        def _():
            act(z - level, True)

        @pl.when(z + level < nz)
        def _():
            act(z + level, False)

    def send_on(src, c, rising):
        if rising:
            @pl.when(z < nz - 1)
            def _():
                hop(src, c, True).start()
        else:
            @pl.when(z > 0)
            def _():
                hop(src, c, False).start()

    own_w = pltpu.make_async_copy(w_ref, w_all.at[dp], own_sem.at[0])
    own_n = pltpu.make_async_copy(n_ref, n_all.at[mine], own_sem.at[1])
    own_w.start()
    own_n.start()
    y_copy(z).start()
    for p in range(nmp - 1):
        m_copy(p).start()
    own_w.wait()
    for c in range(CHUNKS):
        send_on(z, c, True)
        send_on(z, c, False)
        if nx > 1:
            x_copy(z, c).start()

    @pl.loop(1, nz)
    def _(level):
        at_level(level, lambda src, rising: y_copy(src).start())

    acc[...] = jnp.zeros_like(acc)

    def multiply(block):
        cols = pl.ds(pl.multiple_of(block * depth, depth), depth)

        @pl.loop(0, n_all.shape[0])
        def _(i):
            acc[i] += jnp.dot(n_all[i, :, cols], w_all[block], preferred_element_type=jnp.float32)

    def relay(level):
        @pl.loop(0, CHUNKS)
        def _(c):
            def pass_on(src, rising):
                hop(src, c, rising).wait_recv()
                send_on(src, c, rising)
                if nx > 1:
                    x_copy(src, c).start()

            at_level(level, pass_on)

    def share(src):
        y_copy(src).wait_recv()
        for p in range(nmp - 1):
            f_copy(src, p).start()

    def finish(src):
        for p in range(nmp - 1):
            f_copy(src, p).wait_recv()
        multiply(src * nx + x)
        if nx > 1:
            @pl.loop(0, CHUNKS)
            def _(c):
                x_copy(src, c).wait_recv()

            multiply(src * nx + (nx - 1 - x))

    share(z)
    if nz > 1:
        relay(1)
        at_level(1, lambda src, rising: share(src))
    own_n.wait()
    for p in range(nmp - 1):
        m_copy(p).wait_recv()
    finish(z)

    @pl.loop(2, nz)
    def _(level):
        relay(level)
        at_level(level, lambda src, rising: share(src))
        at_level(level - 1, lambda src, rising: finish(src))

    if nz > 1:
        at_level(nz - 1, lambda src, rising: finish(src))
    kvc_ref[...] = acc[...].astype(kvc_ref.dtype)

    @pl.loop(0, nz)
    def _(src):
        @pl.loop(0, CHUNKS)
        def _(c):
            @pl.when((src <= z) & (z < nz - 1))
            def _():
                hop(src, c, True).wait_send()

            @pl.when((src >= z) & (z > 0))
            def _():
                hop(src, c, False).wait_send()

            if nx > 1:
                x_copy(src, c).wait_send()

        y_copy(src).wait_send()
        for p in range(nmp - 1):
            f_copy(src, p).wait_send()

    for p in range(nmp - 1):
        m_copy(p).wait_send()


def project(ndp, nseg, nmp, weight, normed):
    nx = inner_of(ndp)
    nz = ndp // nx
    dma = pltpu.SemaphoreType.DMA
    vmem = pl.BlockSpec(memory_space=pltpu.VMEM)
    rows, width = normed.shape
    cols = weight.shape[1]
    others = max(nmp - 1, 1)
    return pl.pallas_call(
        functools.partial(project_kernel, ndp, nmp),
        out_shape=(
            jax.ShapeDtypeStruct((nseg * nmp, rows, cols), jnp.bfloat16),
            jax.ShapeDtypeStruct((nseg * nmp, rows, width), normed.dtype),
        ),
        in_specs=[vmem, vmem],
        out_specs=(vmem, vmem),
        scratch_shapes=[
            pltpu.VMEM((ndp,) + weight.shape, weight.dtype),
            pltpu.VMEM((nseg * nmp, rows, cols), jnp.float32),
            dma((2,)),
            dma((2, nz, CHUNKS)), dma((nz, CHUNKS)),
            dma((nz, CHUNKS)), dma((nz, CHUNKS)),
            dma((nz,)), dma((nz,)),
            dma((others,)), dma((others,)),
            dma((nz, others)), dma((nz, others)),
        ],
        compiler_params=pltpu.CompilerParams(
            collective_id=0, has_side_effects=True, vmem_limit_bytes=20 * MiB
        ),
        name="project",
    )(weight, normed)


def attention_kernel(
    heads, ratio, kvc, q_ref, akv_ref, go_ref, vis_ref,
    out_ref, dq_ref, dakv_ref, g_ref, pair, grad, sems,
):
    seg = lax.axis_index("segment")
    peer = {"segment": 1 - seg}
    greet([peer])
    give = remote(kvc.at[1 - seg], pair.at[seg], sems.at[0], sems.at[1], peer)
    give.start()
    keep = pltpu.make_async_copy(kvc.at[seg], pair.at[seg], sems.at[2])
    keep.start()
    keep.wait()
    give.wait()
    acts = q_ref.shape[0]
    rows = pair.shape[1]
    scale = HD ** (-0.5)
    vis = vis_ref[...]
    visible = jnp.concatenate([vis] * ratio, axis=0) > 0.5

    def dot(a, b, ca, cb):
        return lax.dot_general(a, b, (((ca,), (cb,)), ((), ())), preferred_element_type=jnp.float32)

    for g in range(heads):
        cols = slice(g * HD, (g + 1) * HD)
        keys = jnp.concatenate([pair[0, :, cols], akv_ref[0, :, cols]], axis=0)
        values = jnp.concatenate([pair[1, :, cols], akv_ref[1, :, cols]], axis=0)
        hs = [slice((g * ratio + r) * HD, (g * ratio + r + 1) * HD) for r in range(ratio)]
        query = jnp.concatenate([q_ref[:, h] for h in hs], axis=0)
        go = jnp.concatenate([go_ref[:, h] for h in hs], axis=0)
        masked = jnp.where(visible, dot(query, keys, 1, 1) * scale, NEGATIVE)
        top = jnp.max(masked, axis=-1, keepdims=True)
        expo = jnp.where(visible, jnp.exp(masked - top), 0.0)
        probs = expo * (1.0 / jnp.sum(expo, axis=-1, keepdims=True))
        low = probs.astype(jnp.bfloat16)
        d_probs = dot(go, values, 1, 1)
        delta = jnp.sum(probs * d_probs, axis=-1, keepdims=True)
        d_scores = (probs * (d_probs - delta)).astype(jnp.bfloat16)
        out = dot(low, values, 1, 0).astype(jnp.bfloat16)
        d_query = dot(d_scores, keys, 1, 0) * scale
        for r, h in enumerate(hs):
            out_ref[:, h] = out[r * acts : (r + 1) * acts]
            dq_ref[:, h] = d_query[r * acts : (r + 1) * acts]
        d_keys = dot(d_scores, query, 0, 0) * scale
        d_values = dot(low, go, 0, 0)
        grad[0, :, cols] = d_keys[:rows].astype(jnp.bfloat16)
        grad[1, :, cols] = d_values[:rows].astype(jnp.bfloat16)
        dakv_ref[0, :, cols] = d_keys[rows:]
        dakv_ref[1, :, cols] = d_values[rows:]
    back = remote(grad.at[1 - seg], g_ref.at[seg], sems.at[3], sems.at[4], peer)
    back.start()
    local = pltpu.make_async_copy(grad.at[seg], g_ref.at[seg], sems.at[5])
    local.start()
    local.wait()
    back.wait()


def attention(heads, ratio, kvc, query, akv, grad_out, visible):
    vmem = pl.BlockSpec(memory_space=pltpu.VMEM)
    acts, width = query.shape
    return pl.pallas_call(
        functools.partial(attention_kernel, heads, ratio),
        out_shape=(
            jax.ShapeDtypeStruct((acts, width), jnp.bfloat16),
            jax.ShapeDtypeStruct((acts, width), jnp.float32),
            jax.ShapeDtypeStruct(akv.shape, jnp.float32),
            jax.ShapeDtypeStruct(kvc.shape, jnp.bfloat16),
        ),
        in_specs=[vmem] * 5,
        out_specs=(vmem,) * 4,
        scratch_shapes=[
            pltpu.VMEM(kvc.shape, jnp.bfloat16),
            pltpu.VMEM(kvc.shape, jnp.bfloat16),
            pltpu.SemaphoreType.DMA((6,)),
        ],
        compiler_params=pltpu.CompilerParams(
            collective_id=1, has_side_effects=True, vmem_limit_bytes=12 * MiB
        ),
        name="attention",
    )(kvc, query, akv, grad_out, visible)


def scatter_kernel(ndp, n_ref, g_ref, o_ref, x_send, x_buf, z_send, z_buf, xs, xr, zs, zr, ys, yr):
    nx = inner_of(ndp)
    nz = ndp // nx
    dp, seg = lax.axis_index("dp"), lax.axis_index("segment")
    z, x = dp // nx, dp % nx
    z_peer = [{"dp": ((z + o) % nz) * nx + x} for o in range(1, nz)]
    x_peer = {"dp": z * nx + (nx - 1 - x)}
    y_peer = {"segment": 1 - seg}
    greet(z_peer + ([x_peer] if nx > 1 else []) + [y_peer])
    order = sorted(range(1, nz), key=lambda o: -min(o, nz - o)) + [0]
    rows = o_ref.shape[1]
    step = min(rows, max(rows // CHUNKS, 128))
    steps = rows // step

    def part(c):
        return pl.ds(pl.multiple_of(c * step, step), step)

    def term(block, c):
        cols = pl.ds(pl.multiple_of(block * rows + c * step, step), step)
        return lax.dot_general(
            n_ref[:, cols], g_ref[...], (((0,), (0,)), ((), ())), preferred_element_type=jnp.float32
        )

    def x_copy(o, c):
        return remote(x_send.at[o, part(c)], x_buf.at[o, part(c)], xs.at[o, c], xr.at[o, c], x_peer)

    def z_copy(o, c):
        return remote(z_send.at[o, part(c)], z_buf.at[o, part(c)], zs.at[o, c], zr.at[o, c], z_peer[o - 1])

    def y_copy(c):
        return remote(o_ref.at[seg, part(c)], o_ref.at[seg, part(c)], ys.at[c], yr.at[c], y_peer)

    if nx > 1:
        for o in order:
            @pl.loop(0, steps)
            def _(c):
                x_send[o, part(c), :] = term(((z + o) % nz) * nx + (nx - 1 - x), c).astype(jnp.bfloat16)
                x_copy(o, c).start()

    for o in order:
        @pl.loop(0, steps)
        def _(c):
            total = term(((z + o) % nz) * nx + x, c)
            if nx > 1:
                x_copy(o, c).wait_recv()
                total = total + x_buf[o, part(c), :].astype(jnp.float32)
            if o > 0:
                z_send[o, part(c), :] = total.astype(jnp.bfloat16)
                z_copy(o, c).start()
            else:
                for other in order[:-1]:
                    z_copy(other, c).wait_recv()
                    total = total + z_buf[other, part(c), :].astype(jnp.float32)
                o_ref[seg, part(c), :] = total.astype(jnp.bfloat16)
                y_copy(c).start()

    @pl.loop(0, steps)
    def _(c):
        y_copy(c).wait()
        for o in order:
            if nx > 1:
                x_copy(o, c).wait_send()
            if o > 0:
                z_copy(o, c).wait_send()


def scatter(ndp, nseg, tokens, grads):
    nx = inner_of(ndp)
    nz = ndp // nx
    dma = pltpu.SemaphoreType.DMA
    vmem = pl.BlockSpec(memory_space=pltpu.VMEM)
    block = (tokens.shape[1] // ndp, grads.shape[1])
    return pl.pallas_call(
        functools.partial(scatter_kernel, ndp),
        out_shape=jax.ShapeDtypeStruct((nseg,) + block, jnp.bfloat16),
        in_specs=[vmem, vmem],
        out_specs=vmem,
        scratch_shapes=[pltpu.VMEM((nz,) + block, jnp.bfloat16)] * 4
        + [dma((nz, CHUNKS))] * 4
        + [dma((CHUNKS,))] * 2,
        compiler_params=pltpu.CompilerParams(
            collective_id=2, has_side_effects=True, vmem_limit_bytes=24 * MiB
        ),
        name="scatter",
    )(tokens, grads)


def shards(
    ndp,
    nseg,
    nmp,
    prefix_hidden,
    norm_gain,
    kv_weight,
    action_query,
    action_kv,
    out_cotangent,
    prefix_blocks,
    action_blocks,
    prefix_lengths,
    timesteps,
):
    heads_kv = kv_weight.shape[2] // HD
    ratio = QH // KVH
    columns = kv_weight.shape[2]
    seg = lax.axis_index("segment")
    wide = prefix_hidden[0].astype(jnp.float32)
    inverse = lax.rsqrt(jnp.mean(wide * wide, axis=-1, keepdims=True) + EPS)
    normed_local = (wide * inverse * norm_gain).astype(jnp.bfloat16)
    own_weight = lax.dynamic_index_in_dim(kv_weight, seg, axis=1, keepdims=False)
    kvc, tokens = project(ndp, nseg, nmp, own_weight, normed_local)
    rows = nmp * normed_local.shape[0]
    width = normed_local.shape[1]
    kvc = kvc.reshape(nseg, rows, columns)
    flow_weight = 0.5 + (timesteps[0].astype(jnp.float32) + 0.5) / STEPS
    grad_out = (flow_weight * out_cotangent[0].astype(jnp.float32)).astype(jnp.bfloat16)
    pblocks = prefix_blocks[0]
    ablocks = action_blocks[0]
    positions = jnp.arange(rows, dtype=jnp.int32)
    see_prefix = (pblocks[None, :] <= ablocks[:, None]) & (positions[None, :] < prefix_lengths[0])
    see_action = ablocks[None, :] <= ablocks[:, None]
    visible = jnp.concatenate([see_prefix, see_action], axis=1).astype(jnp.float32)
    attn_out, query_grad, d_action, grads = attention(
        heads_kv, ratio, kvc, action_query[0], action_kv[0].transpose(1, 0, 2), grad_out, visible
    )
    summed = scatter(
        ndp, nseg, tokens.reshape(nseg * rows, width), grads.reshape(nseg * rows, columns)
    )
    weight_grad = summed.transpose(1, 0, 2).astype(jnp.float32)
    return (attn_out[None], query_grad[None], d_action.transpose(1, 0, 2)[None], weight_grad)


def solution(mesh):
    placed = (
        P(("dp", "segment"), "mp", None),
        P(),
        P("dp", None, "mp"),
        P(("dp", "segment"), None, "mp"),
        P(("dp", "segment"), None, None, "mp"),
        P(("dp", "segment"), None, "mp"),
        P(("dp", "segment"), None),
        P(("dp", "segment"), None),
        P(("dp", "segment")),
        P(("dp", "segment")),
    )
    return jax.shard_map(
        functools.partial(shards, mesh.shape["dp"], mesh.shape["segment"], mesh.shape["mp"]),
        mesh=mesh,
        in_specs=placed,
        out_specs=(
            P(("dp", "segment"), None, "mp"),
            P(("dp", "segment"), None, "mp"),
            P(("dp", "segment"), None, None, "mp"),
            P("dp", None, "mp"),
        ),
        check_vma=False,
    )
```

```python
import functools

import jax
import jax.numpy as jnp
from jax import lax
from jax.experimental import pallas as pl
from jax.experimental.pallas import tpu as pltpu
from jax.sharding import PartitionSpec as P

KVH = 8
HD = 128
QH = 16
STEPS = 1000


EPS = 1e-06
NEGATIVE = -1e30
CHUNKS = 4
MiB = 1 << 20


def inner_of(ndp):
    return 2 if ndp % 2 == 0 else 1


def remote(src, dst, send_sem, recv_sem, where):
    return pltpu.make_async_remote_copy(
        src_ref=src,
        dst_ref=dst,
        send_sem=send_sem,
        recv_sem=recv_sem,
        device_id=where,
        device_id_type=pl.DeviceIdType.MESH,
    )


def greet(peers):
    barrier = pltpu.get_barrier_semaphore()
    for peer in peers:
        pl.semaphore_signal(
            barrier, inc=1, device_id=peer, device_id_type=pl.DeviceIdType.MESH
        )
    pl.semaphore_wait(barrier, len(peers))


def project_kernel(
    ndp, nmp, ns, w_ref, n_ref, *refs
):
    given, (kvc_ref, n_all), taken, rest = refs[:ns], refs[ns : ns + 2], refs[ns + 2 : 2 * ns + 2], refs[2 * ns + 2 :]
    w_all, acc, own_sem, zs, zr, xs, xr, ys, yr, ms, mr, fs, fr, ss, sr = rest
    nx = inner_of(ndp)
    nz = ndp // nx
    dp, seg, mp = lax.axis_index("dp"), lax.axis_index("segment"), lax.axis_index("mp")
    z, x = dp // nx, dp % nx
    z_peer = [{"dp": ((z + o) % nz) * nx + x} for o in range(1, nz)]
    x_peer = {"dp": z * nx + (nx - 1 - x)}
    y_peer = {"segment": 1 - seg}
    m_peer = [{"mp": (mp + o) % nmp} for o in range(1, nmp)]
    greet(z_peer + ([x_peer] if nx > 1 else []) + [y_peer] + m_peer)
    depth = w_ref.shape[0]
    step = depth // CHUNKS
    mine, theirs = seg * nmp + mp, (1 - seg) * nmp + mp
    order = [0] + sorted(range(1, nz), key=lambda o: min(o, nz - o))

    def outer(o):
        return (z + nz - o) % nz

    def columns(o):
        return pl.ds(pl.multiple_of(outer(o) * (nx * depth), nx * depth), nx * depth)

    def z_copy(o, c):
        part = pl.ds(c * step, step)
        return remote(w_ref.at[part], w_all.at[dp, part], zs.at[o - 1, c], zr.at[o - 1, c], z_peer[o - 1])

    def x_copy(o, c):
        part = pl.ds(c * step, step)
        src = outer(o) * nx + x
        held = w_ref.at[part] if o == 0 else w_all.at[src, part]
        return remote(held, w_all.at[src, part], xs.at[o, c], xr.at[o, c], x_peer)

    def y_copy(o):
        return remote(n_ref.at[:, columns(o)], n_all.at[mine, :, columns(o)], ys.at[o], yr.at[o], y_peer)

    def m_copy(p):
        return remote(n_ref, n_all.at[mine], ms.at[p], mr.at[p], m_peer[p])

    def f_copy(o, p):
        part = n_all.at[theirs, :, columns(o)]
        return remote(part, part, fs.at[o, p], fr.at[o, p], m_peer[p])

    own_w = pltpu.make_async_copy(w_ref, w_all.at[dp], own_sem.at[0])
    own_n = pltpu.make_async_copy(n_ref, n_all.at[mine], own_sem.at[1])
    for o in order[1:]:
        for c in range(CHUNKS):
            z_copy(o, c).start()
    if nx > 1:
        for c in range(CHUNKS):
            x_copy(0, c).start()
    for o in order:
        y_copy(o).start()
    for p in range(nmp - 1):
        m_copy(p).start()
    swaps = [
        remote(given[k].at[1 - seg], taken[k], ss.at[k], sr.at[k], y_peer) for k in range(ns)
    ]
    for copy in swaps:
        copy.start()
    own_w.start()
    own_n.start()
    acc[...] = jnp.zeros_like(acc)

    def multiply(block):
        cols = pl.ds(pl.multiple_of(block * depth, depth), depth)

        @pl.loop(0, n_all.shape[0])
        def _(i):
            acc[i] += jnp.dot(n_all[i, :, cols], w_all[block], preferred_element_type=jnp.float32)

    def finish(o):
        for p in range(nmp - 1):
            f_copy(o, p).wait_recv()
        if o == 0:
            own_w.wait()
            own_n.wait()
            for p in range(nmp - 1):
                m_copy(p).wait_recv()
        multiply(outer(o) * nx + x)
        if nx > 1:
            for c in range(CHUNKS):
                x_copy(o, c).wait_recv()
            multiply(outer(o) * nx + (nx - 1 - x))

    for i, o in enumerate(order):
        if o > 0:
            for c in range(CHUNKS):
                z_copy(o, c).wait_recv()
                if nx > 1:
                    x_copy(o, c).start()
        y_copy(o).wait_recv()
        for p in range(nmp - 1):
            f_copy(o, p).start()
        if i > 0:
            finish(order[i - 1])
    finish(order[-1])
    kvc_ref[...] = acc[...].astype(kvc_ref.dtype)
    for copy in swaps:
        copy.wait()
    for o in order:
        if o > 0:
            for c in range(CHUNKS):
                z_copy(o, c).wait_send()
        if nx > 1:
            for c in range(CHUNKS):
                x_copy(o, c).wait_send()
        y_copy(o).wait_send()
        for p in range(nmp - 1):
            f_copy(o, p).wait_send()
    for p in range(nmp - 1):
        m_copy(p).wait_send()


def project(ndp, nseg, nmp, weight, normed, given):
    nx = inner_of(ndp)
    nz = ndp // nx
    dma = pltpu.SemaphoreType.DMA
    vmem = pl.BlockSpec(memory_space=pltpu.VMEM)
    rows, width = normed.shape
    cols = weight.shape[1]
    others, further = max(nmp - 1, 1), max(nz - 1, 1)
    return pl.pallas_call(
        functools.partial(project_kernel, ndp, nmp, len(given)),
        out_shape=(
            jax.ShapeDtypeStruct((nseg * nmp, rows, cols), jnp.bfloat16),
            jax.ShapeDtypeStruct((nseg * nmp, rows, width), normed.dtype),
        )
        + tuple(jax.ShapeDtypeStruct(g.shape[1:], g.dtype) for g in given),
        in_specs=[vmem] * (2 + len(given)),
        out_specs=(vmem,) * (2 + len(given)),
        scratch_shapes=[
            pltpu.VMEM((ndp,) + weight.shape, weight.dtype),
            pltpu.VMEM((nseg * nmp, rows, cols), jnp.float32),
            dma((2,)),
            dma((further, CHUNKS)), dma((further, CHUNKS)),
            dma((nz, CHUNKS)), dma((nz, CHUNKS)),
            dma((nz,)), dma((nz,)),
            dma((others,)), dma((others,)),
            dma((nz, others)), dma((nz, others)),
            dma((max(len(given), 1),)), dma((max(len(given), 1),)),
        ],
        compiler_params=pltpu.CompilerParams(
            collective_id=0, has_side_effects=True, vmem_limit_bytes=20 * MiB
        ),
        name="project",
    )(weight, normed, *given)


def attention_kernel(
    heads, ratio, kvc, q_ref, akv_ref, go_ref, vis_ref,
    out_ref, dq_ref, dakv_ref, g_ref, pair, grad, sems,
):
    seg = lax.axis_index("segment")
    peer = {"segment": 1 - seg}
    greet([peer])
    give = remote(kvc.at[1 - seg], pair.at[seg], sems.at[0], sems.at[1], peer)
    give.start()
    keep = pltpu.make_async_copy(kvc.at[seg], pair.at[seg], sems.at[2])
    keep.start()
    keep.wait()
    give.wait()
    acts = q_ref.shape[0]
    rows = pair.shape[1]
    scale = HD ** (-0.5)
    vis = vis_ref[...]
    visible = jnp.concatenate([vis] * ratio, axis=0) > 0.5

    def dot(a, b, ca, cb):
        return lax.dot_general(a, b, (((ca,), (cb,)), ((), ())), preferred_element_type=jnp.float32)

    for g in range(heads):
        cols = slice(g * HD, (g + 1) * HD)
        keys = jnp.concatenate([pair[0, :, cols], akv_ref[0, :, cols]], axis=0)
        values = jnp.concatenate([pair[1, :, cols], akv_ref[1, :, cols]], axis=0)
        hs = [slice((g * ratio + r) * HD, (g * ratio + r + 1) * HD) for r in range(ratio)]
        query = jnp.concatenate([q_ref[:, h] for h in hs], axis=0)
        go = jnp.concatenate([go_ref[:, h] for h in hs], axis=0)
        masked = jnp.where(visible, dot(query, keys, 1, 1) * scale, NEGATIVE)
        top = jnp.max(masked, axis=-1, keepdims=True)
        expo = jnp.where(visible, jnp.exp(masked - top), 0.0)
        probs = expo * (1.0 / jnp.sum(expo, axis=-1, keepdims=True))
        low = probs.astype(jnp.bfloat16)
        d_probs = dot(go, values, 1, 1)
        delta = jnp.sum(probs * d_probs, axis=-1, keepdims=True)
        d_scores = (probs * (d_probs - delta)).astype(jnp.bfloat16)
        out = dot(low, values, 1, 0).astype(jnp.bfloat16)
        d_query = dot(d_scores, keys, 1, 0) * scale
        for r, h in enumerate(hs):
            out_ref[:, h] = out[r * acts : (r + 1) * acts]
            dq_ref[:, h] = d_query[r * acts : (r + 1) * acts]
        d_keys = dot(d_scores, query, 0, 0) * scale
        d_values = dot(low, go, 0, 0)
        grad[0, :, cols] = d_keys[:rows].astype(jnp.bfloat16)
        grad[1, :, cols] = d_values[:rows].astype(jnp.bfloat16)
        dakv_ref[0, :, cols] = d_keys[rows:]
        dakv_ref[1, :, cols] = d_values[rows:]
    back = remote(grad.at[1 - seg], g_ref.at[seg], sems.at[3], sems.at[4], peer)
    back.start()
    local = pltpu.make_async_copy(grad.at[seg], g_ref.at[seg], sems.at[5])
    local.start()
    local.wait()
    back.wait()


def attention(heads, ratio, kvc, query, akv, grad_out, visible):
    vmem = pl.BlockSpec(memory_space=pltpu.VMEM)
    acts, width = query.shape
    return pl.pallas_call(
        functools.partial(attention_kernel, heads, ratio),
        out_shape=(
            jax.ShapeDtypeStruct((acts, width), jnp.bfloat16),
            jax.ShapeDtypeStruct((acts, width), jnp.float32),
            jax.ShapeDtypeStruct(akv.shape, jnp.float32),
            jax.ShapeDtypeStruct(kvc.shape, jnp.bfloat16),
        ),
        in_specs=[vmem] * 5,
        out_specs=(vmem,) * 4,
        scratch_shapes=[
            pltpu.VMEM(kvc.shape, jnp.bfloat16),
            pltpu.VMEM(kvc.shape, jnp.bfloat16),
            pltpu.SemaphoreType.DMA((6,)),
        ],
        compiler_params=pltpu.CompilerParams(
            collective_id=1, has_side_effects=True, vmem_limit_bytes=12 * MiB
        ),
        name="attention",
    )(kvc, query, akv, grad_out, visible)


def scatter_kernel(ndp, ns, n_ref, g_ref, *refs):
    given, o_ref, whole, rest = refs[:ns], refs[ns], refs[ns + 1 : 2 * ns + 1], refs[2 * ns + 1 :]
    x_send, x_buf, z_send, z_buf, xs, xr, zs, zr, ys, yr, ss = rest
    nx = inner_of(ndp)
    nz = ndp // nx
    dp, seg = lax.axis_index("dp"), lax.axis_index("segment")
    z, x = dp // nx, dp % nx
    z_peer = [{"dp": ((z + o) % nz) * nx + x} for o in range(1, nz)]
    x_peer = {"dp": z * nx + (nx - 1 - x)}
    y_peer = {"segment": 1 - seg}
    greet(z_peer + ([x_peer] if nx > 1 else []) + [y_peer])
    order = sorted(range(1, nz), key=lambda o: -min(o, nz - o)) + [0]
    rows = o_ref.shape[1]
    step = min(rows, max(rows // CHUNKS, 128))
    steps = rows // step

    def part(c):
        return pl.ds(pl.multiple_of(c * step, step), step)

    def term(block, c):
        cols = pl.ds(pl.multiple_of(block * rows + c * step, step), step)
        return lax.dot_general(
            n_ref[:, cols], g_ref[...], (((0,), (0,)), ((), ())), preferred_element_type=jnp.float32
        )

    def x_copy(o, c):
        return remote(x_send.at[o, part(c)], x_buf.at[o, part(c)], xs.at[o, c], xr.at[o, c], x_peer)

    def z_copy(o, c):
        return remote(z_send.at[o, part(c)], z_buf.at[o, part(c)], zs.at[o, c], zr.at[o, c], z_peer[o - 1])

    def y_copy(c):
        return remote(o_ref.at[seg, part(c)], o_ref.at[seg, part(c)], ys.at[c], yr.at[c], y_peer)

    swaps = [
        remote(given[k].at[1], whole[k].at[seg], ss.at[0, k], ss.at[1, k], y_peer) for k in range(ns)
    ]
    keeps = [pltpu.make_async_copy(given[k].at[0], whole[k].at[seg], ss.at[2, k]) for k in range(ns)]
    for copy in swaps + keeps:
        copy.start()

    if nx > 1:
        for o in order:
            @pl.loop(0, steps)
            def _(c):
                x_send[o, part(c), :] = term(((z + o) % nz) * nx + (nx - 1 - x), c).astype(jnp.bfloat16)
                x_copy(o, c).start()

    for o in order:
        @pl.loop(0, steps)
        def _(c):
            total = term(((z + o) % nz) * nx + x, c)
            if nx > 1:
                x_copy(o, c).wait_recv()
                total = total + x_buf[o, part(c), :].astype(jnp.float32)
            if o > 0:
                z_send[o, part(c), :] = total.astype(jnp.bfloat16)
                z_copy(o, c).start()
            else:
                for other in order[:-1]:
                    z_copy(other, c).wait_recv()
                    total = total + z_buf[other, part(c), :].astype(jnp.float32)
                o_ref[seg, part(c), :] = total.astype(jnp.bfloat16)
                y_copy(c).start()

    for copy in swaps + keeps:
        copy.wait()

    @pl.loop(0, steps)
    def _(c):
        y_copy(c).wait()
        for o in order:
            if nx > 1:
                x_copy(o, c).wait_send()
            if o > 0:
                z_copy(o, c).wait_send()


def scatter(ndp, nseg, tokens, grads, given):
    nx = inner_of(ndp)
    nz = ndp // nx
    dma = pltpu.SemaphoreType.DMA
    vmem = pl.BlockSpec(memory_space=pltpu.VMEM)
    block = (tokens.shape[1] // ndp, grads.shape[1])
    return pl.pallas_call(
        functools.partial(scatter_kernel, ndp, len(given)),
        out_shape=(jax.ShapeDtypeStruct((nseg,) + block, jnp.bfloat16),)
        + tuple(jax.ShapeDtypeStruct(g.shape, g.dtype) for g in given),
        in_specs=[vmem] * (2 + len(given)),
        out_specs=(vmem,) * (1 + len(given)),
        scratch_shapes=[pltpu.VMEM((nz,) + block, jnp.bfloat16)] * 4
        + [dma((nz, CHUNKS))] * 4
        + [dma((CHUNKS,))] * 2
        + [dma((3, max(len(given), 1)))],
        compiler_params=pltpu.CompilerParams(
            collective_id=2, has_side_effects=True, vmem_limit_bytes=24 * MiB
        ),
        name="scatter",
    )(tokens, grads, *given)


def local_attention_kernel(heads, ratio, kvc, pack, code, pack_in, code_in, _, out_ref, dq_ref, dakv_ref, g_ref):
    seg = lax.axis_index("segment")
    acts = pack.shape[2]
    rows = kvc.shape[1]
    width = heads * HD
    scale = HD ** (-0.5)

    def dot(a, b, ca, cb):
        return lax.dot_general(a, b, (((ca,), (cb,)), ((), ())), preferred_element_type=jnp.float32)

    for t in range(2):
        sample = seg if t == 0 else 1 - seg

        def held(k, cols):
            return pack[seg, k, :, cols] if t == 0 else pack_in[k, :, cols]

        line = code[0, 0:1, :] if t == 0 else code_in[0:1, :]
        level = jnp.broadcast_to(line[:, rows:], (acts, acts)).T
        tiles = [
            jnp.where(line[:, i * acts : (i + 1) * acts] <= level, 1.0, 0.0)
            for i in range((rows + acts) // acts)
        ]
        visible = jnp.concatenate([jnp.concatenate(tiles, axis=1)] * ratio, axis=0) > 0.5
        for g in range(heads):
            kc, vc = slice(g * HD, (g + 1) * HD), slice(width + g * HD, width + (g + 1) * HD)
            keys = jnp.concatenate([kvc[sample, :, kc], held(2, kc)], axis=0)
            values = jnp.concatenate([kvc[sample, :, vc], held(2, vc)], axis=0)
            hs = [slice((g * ratio + r) * HD, (g * ratio + r + 1) * HD) for r in range(ratio)]
            query = jnp.concatenate([held(0, h) for h in hs], axis=0)
            go = jnp.concatenate([held(1, h) for h in hs], axis=0)
            masked = jnp.where(visible, dot(query, keys, 1, 1) * scale, NEGATIVE)
            top = jnp.max(masked, axis=-1, keepdims=True)
            expo = jnp.where(visible, jnp.exp(masked - top), 0.0)
            probs = expo * (1.0 / jnp.sum(expo, axis=-1, keepdims=True))
            low = probs.astype(jnp.bfloat16)
            d_probs = dot(go, values, 1, 1)
            delta = jnp.sum(probs * d_probs, axis=-1, keepdims=True)
            d_scores = (probs * (d_probs - delta)).astype(jnp.bfloat16)
            out = dot(low, values, 1, 0).astype(jnp.bfloat16)
            d_query = dot(d_scores, keys, 1, 0) * scale
            for r, h in enumerate(hs):
                out_ref[t, :, h] = out[r * acts : (r + 1) * acts]
                dq_ref[t, :, h] = d_query[r * acts : (r + 1) * acts]
            d_keys = dot(d_scores, query, 0, 0) * scale
            d_values = dot(low, go, 0, 0)
            g_ref[sample, :, kc] = d_keys[:rows].astype(jnp.bfloat16)
            g_ref[sample, :, vc] = d_values[:rows].astype(jnp.bfloat16)
            dakv_ref[t, :, kc] = d_keys[rows:]
            dakv_ref[t, :, vc] = d_values[rows:]


def local_attention(heads, ratio, kvc, pack, code, pack_in, code_in, tokens):
    vmem = pl.BlockSpec(memory_space=pltpu.VMEM)
    nseg, _, acts, width = pack.shape
    return pl.pallas_call(
        functools.partial(local_attention_kernel, heads, ratio),
        out_shape=(
            jax.ShapeDtypeStruct((nseg, acts, width), jnp.bfloat16),
            jax.ShapeDtypeStruct((nseg, acts, width), jnp.float32),
            jax.ShapeDtypeStruct((nseg, acts, width), jnp.float32),
            jax.ShapeDtypeStruct(kvc.shape, jnp.bfloat16),
        ),
        in_specs=[vmem] * 5 + [pl.BlockSpec(memory_space=pl.ANY)],
        out_specs=(vmem,) * 4,
        compiler_params=pltpu.CompilerParams(vmem_limit_bytes=8 * MiB),
        name="local_attention",
    )(kvc, pack, code, pack_in, code_in, tokens)


def by_heads(ndp, nseg, nmp, weight, normed, query, akv, grad_out, pblocks, ablocks, length):
    acts = query.shape[0]
    depth, _, columns = weight.shape
    part = columns // nseg
    heads, ratio = part // HD, QH // KVH
    rows = nmp * normed.shape[0]
    width = normed.shape[1]
    seg = lax.axis_index("segment")
    own_weight = lax.dynamic_slice_in_dim(weight, seg * part, part, axis=2).reshape(depth, 2 * part)
    pack = jnp.stack(
        [
            query.reshape(acts, nseg, 2 * part),
            grad_out.reshape(acts, nseg, 2 * part),
            akv.reshape(acts, 2, nseg, part).transpose(0, 2, 1, 3).reshape(acts, nseg, 2 * part),
        ]
    ).transpose(2, 0, 1, 3)
    positions = jnp.arange(rows, dtype=jnp.int32)
    seen_from = jnp.where(positions < length, pblocks.astype(jnp.float32), 1e9)
    code = jnp.concatenate([seen_from, ablocks.astype(jnp.float32)])
    code = jnp.broadcast_to(code, (nseg, 8, code.shape[0]))
    kvc, tokens, pack_in, code_in = project(ndp, nseg, nmp, own_weight, normed, (pack, code))
    out, d_query, d_action, grads = local_attention(
        heads, ratio, kvc.reshape(nseg, rows, 2 * part), pack, code, pack_in, code_in, tokens
    )
    summed, out, d_query, d_action = scatter(
        ndp,
        nseg,
        tokens.reshape(nseg * rows, width),
        grads.reshape(nseg * rows, 2 * part),
        (out, d_query, d_action),
    )
    attn_out = out.transpose(1, 0, 2).reshape(acts, nseg * 2 * part)
    query_grad = d_query.transpose(1, 0, 2).reshape(acts, nseg * 2 * part)
    d_action = d_action.reshape(nseg, acts, 2, part).transpose(1, 2, 0, 3).reshape(acts, 2, columns)
    weight_grad = summed.reshape(nseg, depth, 2, part).transpose(1, 2, 0, 3).reshape(depth, 2, columns)
    return (attn_out[None], query_grad[None], d_action[None], weight_grad.astype(jnp.float32))


def shards(
    ndp,
    nseg,
    nmp,
    prefix_hidden,
    norm_gain,
    kv_weight,
    action_query,
    action_kv,
    out_cotangent,
    prefix_blocks,
    action_blocks,
    prefix_lengths,
    timesteps,
):
    heads_kv = kv_weight.shape[2] // HD
    ratio = QH // KVH
    columns = kv_weight.shape[2]
    seg = lax.axis_index("segment")
    wide = prefix_hidden[0].astype(jnp.float32)
    inverse = lax.rsqrt(jnp.mean(wide * wide, axis=-1, keepdims=True) + EPS)
    normed_local = (wide * inverse * norm_gain).astype(jnp.bfloat16)
    flow_weight = 0.5 + (timesteps[0].astype(jnp.float32) + 0.5) / STEPS
    grad_out = (flow_weight * out_cotangent[0].astype(jnp.float32)).astype(jnp.bfloat16)
    if ratio == 2 and heads_kv % nseg == 0:
        return by_heads(
            ndp, nseg, nmp, kv_weight, normed_local, action_query[0], action_kv[0], grad_out,
            prefix_blocks[0], action_blocks[0], prefix_lengths[0],
        )
    own_weight = lax.dynamic_index_in_dim(kv_weight, seg, axis=1, keepdims=False)
    kvc, tokens = project(ndp, nseg, nmp, own_weight, normed_local, ())
    rows = nmp * normed_local.shape[0]
    width = normed_local.shape[1]
    kvc = kvc.reshape(nseg, rows, columns)
    pblocks = prefix_blocks[0]
    ablocks = action_blocks[0]
    positions = jnp.arange(rows, dtype=jnp.int32)
    see_prefix = (pblocks[None, :] <= ablocks[:, None]) & (positions[None, :] < prefix_lengths[0])
    see_action = ablocks[None, :] <= ablocks[:, None]
    visible = jnp.concatenate([see_prefix, see_action], axis=1).astype(jnp.float32)
    attn_out, query_grad, d_action, grads = attention(
        heads_kv, ratio, kvc, action_query[0], action_kv[0].transpose(1, 0, 2), grad_out, visible
    )
    (summed,) = scatter(
        ndp, nseg, tokens.reshape(nseg * rows, width), grads.reshape(nseg * rows, columns), ()
    )
    weight_grad = summed.transpose(1, 0, 2).astype(jnp.float32)
    return (attn_out[None], query_grad[None], d_action.transpose(1, 0, 2)[None], weight_grad)


def solution(mesh):
    placed = (
        P(("dp", "segment"), "mp", None),
        P(),
        P("dp", None, "mp"),
        P(("dp", "segment"), None, "mp"),
        P(("dp", "segment"), None, None, "mp"),
        P(("dp", "segment"), None, "mp"),
        P(("dp", "segment"), None),
        P(("dp", "segment"), None),
        P(("dp", "segment")),
        P(("dp", "segment")),
    )
    return jax.shard_map(
        functools.partial(shards, mesh.shape["dp"], mesh.shape["segment"], mesh.shape["mp"]),
        mesh=mesh,
        in_specs=placed,
        out_specs=(
            P(("dp", "segment"), None, "mp"),
            P(("dp", "segment"), None, "mp"),
            P(("dp", "segment"), None, None, "mp"),
            P("dp", None, "mp"),
        ),
        check_vma=False,
    )
```
